256 devices in a mesh: grp: 8 (over z), ep: 32 (over y, x, core).
Axes of the slice: x: 4, y: 4, z: 8, core: 2. Of those that a mesh axis runs over, the one named last changes fastest.
Arguments:
- pol_hidden: bfloat16 [10240, 1024], P(('grp', 'ep')), may hold values from -80 to 80
- ref_hidden: bfloat16 [10240, 1024], P(('grp', 'ep')), may hold values from -80 to 80
- pol_routes: int32 [10240, 8], P(('grp', 'ep')), may hold values from 0 to 63, all different within a row; in each aligned block of 40 rows (0 to 39, 40 to 79, ...) at most 7 rows name the same one
- ref_routes: int32 [10240, 8], P(('grp', 'ep')), may hold values from 0 to 63, all different within a row; in each aligned block of 40 rows (0 to 39, 40 to 79, ...) at most 7 rows name the same one
- pol_gates: float32 [10240, 8], P(('grp', 'ep')), may hold values from 0.02 to 0.3
- ref_gates: float32 [10240, 8], P(('grp', 'ep')), may hold values from 0.02 to 0.3
- w_gate: bfloat16 [64, 1024, 384], P('ep'), may hold values from -0.1875 to 0.1875
- w_up: bfloat16 [64, 1024, 384], P('ep'), may hold values from -0.1875 to 0.1875
- w_down: bfloat16 [64, 384, 1024], P('ep'), may hold values from -0.3125 to 0.3125
- norm_gain: float32 [1024], replicated, may hold values from 0.5 to 1.5
- vocab_head: bfloat16 [77824, 1024], P(('grp', 'ep')), may hold values from -2 to 2
- targets: int32 [10240], P(('grp', 'ep')), may hold values from 0 to 77823
- seq_lengths: int32 [256], replicated, may hold values from 1 to 1024, 10240 in all
- owners: int32 [256], replicated, may hold values from 0 to 255, each once
Outputs:
- token_ratio: float32 [10240], P(('grp', 'ep'))
- owned_mean: float32 [256], P(('grp', 'ep'))
The draws below stay inside these ranges and needn't reach their ends.
Inputs may be any that keep to these rules, and one draw needn't show every extreme that they name: `pol_routes`: each row names 8 different experts; among the 40 rows of one device no expert is named by more than 7 rows, a bound that some block reaches. `ref_routes`: each row names 8 different experts; among the 40 rows of one device no expert is named by more than 7 rows, a bound that some block reaches. `seq_lengths`: the lengths sum to 10240; the longest is exactly 1024. `owners`: every device index appears exactly once.
All inputs are finite; a program needn't handle non-finite values.
Results may differ from the reference program's by a relative error of at most 0.0062.
Values may be sent and summed in bfloat16 or wider, within the bound.
A program may use at most 128 MiB of HBM per device.

```python
import math
import jax
import jax.numpy as jnp
import numpy as np
from jax import lax

D = 1024
TOP = 8
FF = 384
EXPERTS = 64
VOCAB = 77824
TOK_DEV = 40
TOKENS = 10240
SEQS = 256
MOST_LEN = 1024
CAP = 7


def hidden_law(key, salt):
    inner_key = jax.random.fold_in(key, salt)
    key_base, key_rows, key_cols = jax.random.split(inner_key, 3)
    row_scale = jnp.exp(jax.random.uniform(key_rows, (TOKENS, 1), jnp.float32, math.log(0.5), math.log(5.0)))
    col_scale = jnp.exp(jax.random.uniform(key_cols, (1, D), jnp.float32, math.log(0.3), math.log(3.0)))
    base = jnp.clip(jax.random.normal(key_base, (TOKENS, D), jnp.float32), -4.0, 4.0)
    values = base * row_scale * col_scale
    return values.astype(jnp.bfloat16)


def draw_pol_hidden(key, part):
    return hidden_law(key, 11)


def draw_ref_hidden(key, part):
    return hidden_law(key, 12)


def draw_vocab_head(key, part):
    inner_key = jax.random.fold_in(key, 21)
    key_base, key_rows = jax.random.split(inner_key, 2)
    row_scale = jnp.exp(jax.random.uniform(key_rows, (VOCAB, 1), jnp.float32, 0.0, math.log(10.0))) * D ** (-0.5)
    values = jnp.clip(jax.random.normal(key_base, (VOCAB, D), jnp.float32), -4.0, 4.0) * row_scale
    return values.astype(jnp.bfloat16)


def place_ends(drawn, stream_key, smallest, largest):
    dims = drawn.shape
    spot = [jax.random.randint(jax.random.fold_in(stream_key, axis), (), 0, dims[axis]) for axis in range(len(dims))]
    drawn = drawn.at[tuple(spot)].set(smallest)
    longest = dims.index(max(dims))
    spot[longest] = (spot[longest] + 1) % dims[longest]
    return drawn.at[tuple(spot)].set(largest)


def shard_levels(stream_key, shape, cuts, least, high):
    level = 1.0
    for position, parts in cuts:
        steps = jax.random.uniform(jax.random.fold_in(jax.random.fold_in(stream_key, 6), position), (parts,), jnp.float32, least / len(cuts), high / len(cuts))
        level = level * jnp.repeat(jnp.exp(steps), shape[position] // parts).reshape((-1,) + (1,) * (len(shape) - 1 - position))
    return level


def skewed_wide(own_key, extent, amount, slope):
    portions = [min(1 << octave, amount + 1 - (1 << octave)) * (1 << 20) // math.isqrt((1 << octave) ** slope) + 1 for octave in range((amount + 1).bit_length()) if 1 << octave <= amount]
    deviation = 1 + sum(portions) // (1 << 30)
    listing = np.cumsum(np.array([max(1, weight // deviation) for weight in portions]))
    lot = jax.random.randint(jax.random.fold_in(own_key, 1), extent, 0, int(listing[len(portions) - 1]))
    start = jnp.left_shift(1, jnp.searchsorted(jnp.asarray(listing, jnp.int32), lot, side="right").astype(jnp.int32))
    standing = start - 1 + jax.random.randint(jax.random.fold_in(own_key, 4), extent, 0, 1 << 30) % jnp.minimum(start, amount + 1 - start)
    return jax.random.permutation(jax.random.fold_in(own_key, 2), amount)[standing].astype(jnp.int32)


def split_up(number_of, total, limit, skew):
    weights = [(1 << 20) // math.isqrt(grade ** skew) + 1 for grade in range(2, number_of + 1)]
    spare, counts = total - limit - (number_of - 1), [1] * (number_of - 1)
    while spare > 0:
        movable = [i for i in range(number_of - 1) if counts[i] < limit]
        whole, budget = sum([weights[i] for i in movable]), spare
        for i in movable:
            more = min(limit - counts[i], max(1, budget * weights[i] // whole), spare)
            counts[i] = counts[i] + more
            spare = spare - more
    return np.array([limit] + counts)


def ragged_sizes(key, number_of, total, bound, skew):
    if number_of == 2:
        one = jax.random.randint(key, (), max(1, total - bound), min(bound, total - 1) + 1)
        return jnp.stack([one, total - one])
    lengths = jnp.asarray(split_up(number_of, total, bound, skew), jnp.int32)
    twos = (number_of - 1) // 2
    giver, receiver = lengths[1:1 + 2 * twos:2], lengths[2:2 + 2 * twos:2]
    slack = jnp.minimum(giver - 1, bound - receiver)
    passed = jax.random.randint(jax.random.fold_in(key, 1), (twos,), 0, 1 << 20) % (slack + 1)
    lengths = lengths.at[1:1 + 2 * twos:2].set(giver - passed).at[2:2 + 2 * twos:2].set(receiver + passed)
    return lengths[jax.random.permutation(jax.random.fold_in(key, 2), number_of)]


def shared_out(rng, own, number, rows, count, top, bound, lean):
    order = jax.random.permutation(rng, count)
    packed, ordinary = load_shares(count, rows * top, bound, lean, True), load_shares(count, rows * top, bound, lean, False)
    places = jnp.arange(count)

    def named(tallies, offset_by):
        used = int((tallies > 0).sum())
        fixed = max(1, used // 4)
        shifted = fixed + (places - fixed + offset_by * (used - fixed)) % max(1, count - fixed)
        return jnp.zeros((count,), jnp.int32).at[order[jnp.where(places < fixed, places, shifted)]].set(jnp.asarray(tallies, jnp.int32))

    tallies = jnp.where(number % 4 == 0, named(packed, number // 4), named(ordinary, number - number // 4 - 1))
    mixed = jax.random.permutation(jax.random.fold_in(own, 3), count)
    donor, sink = mixed[0:count // 2 * 2:2], mixed[1:count // 2 * 2:2]
    slack = jnp.minimum(tallies[donor] - 1, bound - tallies[sink]) // 2
    slack = jnp.where((donor == order[0]) | (sink == order[0]) | (tallies[sink] == 0), 0, jnp.maximum(slack, 0))
    shifted = jax.random.randint(jax.random.fold_in(own, 4), (count // 2,), 0, 1 << 20) % (slack + 1)
    tallies = tallies.at[donor].add(-shifted).at[sink].add(shifted)
    labels = jnp.searchsorted(jnp.cumsum(tallies), jnp.arange(rows * top), side="right").astype(jnp.int32)
    table = labels.reshape(top, rows).T
    table = table[jax.random.permutation(jax.random.fold_in(own, 1), rows)]
    offset_by = jax.random.randint(jax.random.fold_in(own, 2), (rows, 1), 0, top)
    return jnp.take_along_axis(table, (jnp.arange(top)[None, :] + offset_by) % top, axis=1)


def load_shares(amount, total, most, skew, full):
    loads = [(1 << 20) // math.isqrt(rank ** skew) + 1 for rank in range(1, amount + 1)]
    largest = most if full else min(most, max(-(-total // amount), total * loads[0] // sum(loads)))
    least = 1 if total - largest >= amount - 1 else 0
    given, rest = [largest] + [least] * (amount - 1), total - largest - least * (amount - 1)
    while rest > 0:
        movable = [i for i in range(1, amount) if given[i] < largest] or [i for i in range(1, amount) if given[i] < most]
        whole, budget = sum([loads[i] for i in movable]), rest
        for i in movable:
            more = min(most - given[i], max(1, budget * loads[i] // whole), rest)
            given[i] = given[i] + more
            rest = rest - more
    return np.array(given)


def bell_draw(own_key, dims, spread, bound, pieces=(), kind=jnp.bfloat16):
    drawn = jax.random.normal(own_key, dims, jnp.float32) * spread
    if len(pieces) > 0:
        drawn = shard_levels(own_key, dims, pieces, -0.22, 0.18) * drawn
    return jnp.clip(drawn, min=-bound, max=bound).astype(kind)


def setup_inputs(seed: int = 0) -> dict:
    seeds = jax.random.split(jax.random.key(seed), 15)
    pol_hidden = draw_pol_hidden(jax.random.fold_in(seeds[14], 71), 0)
    ref_hidden = draw_ref_hidden(jax.random.fold_in(seeds[14], 71), 0)
    pol_routes_keys = jax.random.split(jax.random.fold_in(seeds[2], 1), TOKENS // TOK_DEV)
    pol_routes_turns = jax.random.permutation(jax.random.fold_in(seeds[2], 3), TOKENS // TOK_DEV)
    pol_routes = jax.vmap(lambda own, number: shared_out(jax.random.fold_in(seeds[2], 2), own, number, TOK_DEV, EXPERTS, TOP, CAP, 2))(pol_routes_keys, pol_routes_turns).reshape((TOKENS, TOP))
    ref_routes_keys = jax.random.split(jax.random.fold_in(seeds[3], 1), TOKENS // TOK_DEV)
    ref_routes_turns = jax.random.permutation(jax.random.fold_in(seeds[3], 3), TOKENS // TOK_DEV)
    ref_routes = jax.vmap(lambda own, number: shared_out(jax.random.fold_in(seeds[3], 2), own, number, TOK_DEV, EXPERTS, TOP, CAP, 2))(ref_routes_keys, ref_routes_turns).reshape((TOKENS, TOP))
    pol_gates = jnp.clip(jnp.exp(math.log(0.3) - 2.7080503 * jax.random.uniform(seeds[4], (TOKENS, TOP), jnp.float32) ** shard_levels(seeds[4], (TOKENS, TOP), ((0, 256),), -0.2, 0.2)), 0.02, 0.3)
    ref_gates = jnp.clip(jnp.exp(math.log(0.3) - 2.7080503 * jax.random.uniform(seeds[5], (TOKENS, TOP), jnp.float32) ** shard_levels(seeds[5], (TOKENS, TOP), ((0, 256),), -0.2, 0.2)), 0.02, 0.3)
    w_gate = bell_draw(seeds[6], (EXPERTS, D, FF), D ** -0.5, 0.1875, ((0, 32),))
    w_up = bell_draw(seeds[7], (EXPERTS, D, FF), D ** -0.5, 0.1875, ((0, 32),))
    w_down = bell_draw(seeds[8], (EXPERTS, FF, D), FF ** -0.5, 0.3125, ((0, 32),))
    norm_gain = jnp.clip(1.0 + 0.1 * jax.random.normal(seeds[9], (D,), jnp.float32), 0.5, 1.5)
    vocab_head = draw_vocab_head(jax.random.fold_in(seeds[14], 71), 0)
    targets = place_ends(skewed_wide(seeds[11], (TOKENS,), VOCAB, 2), jax.random.fold_in(seeds[11], 3), 0, VOCAB - 1).astype(jnp.int32)
    seq_lengths = ragged_sizes(seeds[12], SEQS, TOKENS, MOST_LEN, 2).astype(jnp.int32)
    owners = jax.random.permutation(seeds[13], SEQS).astype(jnp.int32)
    return {"pol_hidden": pol_hidden, "ref_hidden": ref_hidden, "pol_routes": pol_routes, "ref_routes": ref_routes, "pol_gates": pol_gates, "ref_gates": ref_gates, "w_gate": w_gate, "w_up": w_up, "w_down": w_down, "norm_gain": norm_gain, "vocab_head": vocab_head, "targets": targets, "seq_lengths": seq_lengths, "owners": owners}


def expert_layer(hidden, routes, gates, w_gate, w_up, w_down):

    def one_expert(carry, items):
        gate_w, up_w, down_w, expert_id = items
        gate_act = jnp.dot(hidden, gate_w, preferred_element_type=jnp.float32)
        up_act = jnp.dot(hidden, up_w, preferred_element_type=jnp.float32)
        inner = (jax.nn.silu(gate_act) * up_act).astype(jnp.bfloat16)
        output = jnp.dot(inner, down_w, preferred_element_type=jnp.float32).astype(jnp.bfloat16)
        weight = lax.optimization_barrier(jnp.sum(jnp.where(routes == expert_id, gates, jnp.zeros_like(gates)), axis=1))
        return (carry + weight[:, None] * output.astype(gates.dtype), None)
    start_value = hidden.astype(gates.dtype)
    expert_ids = jnp.arange(w_gate.shape[0], dtype=jnp.int32)
    mixed, unused = lax.scan(one_expert, start_value, (w_gate, w_up, w_down, expert_ids))
    return mixed

def log_probs(normed, vocab_head, wanted):
    total_rows = normed.shape[0]
    block_rows = math.gcd(total_rows, 256)
    blocks = normed.reshape(total_rows // block_rows, block_rows, normed.shape[1])
    wanted_blocks = wanted.reshape(total_rows // block_rows, block_rows)

    def one_block(items):
        row_block, wanted_block = items
        logits = jnp.dot(row_block, vocab_head.T, preferred_element_type=jnp.float32)
        peak = lax.optimization_barrier(jnp.max(logits, axis=1))
        lse = peak + jnp.log(lax.optimization_barrier(jnp.sum(jnp.exp(logits - peak[:, None]), axis=1)))
        picked = jnp.take_along_axis(logits, wanted_block[:, None], axis=1)[:, 0]
        return picked - lse
    return lax.map(one_block, (blocks, wanted_blocks)).reshape(total_rows)

def reference(pol_hidden, ref_hidden, pol_routes, ref_routes, pol_gates, ref_gates, w_gate, w_up, w_down, norm_gain, vocab_head, targets, seq_lengths, owners):
    hidden = jnp.concatenate((pol_hidden, ref_hidden), axis=0)
    routes = jnp.concatenate((pol_routes, ref_routes), axis=0)
    gates = jnp.concatenate((pol_gates, ref_gates), axis=0)
    mixed = expert_layer(hidden, routes, gates, w_gate, w_up, w_down)
    scale = lax.rsqrt(lax.optimization_barrier(jnp.mean(mixed * mixed, axis=1, keepdims=True)) + 1e-06)
    normed = (mixed * scale * norm_gain).astype(jnp.bfloat16)
    wanted = jnp.concatenate((targets, targets), axis=0)
    logprob = log_probs(normed, vocab_head, wanted)
    token_ratio = logprob[:TOKENS] - logprob[TOKENS:]
    offsets = jnp.cumsum(seq_lengths) - seq_lengths
    positions = jnp.arange(TOKENS, dtype=jnp.int32)
    segment_ids = (lax.optimization_barrier(jnp.sum((positions[:, None] >= offsets[None, :]).astype(jnp.int32), axis=1)) - 1).astype(jnp.int32)
    sums = jax.ops.segment_sum(token_ratio, segment_ids, num_segments=SEQS)
    means = sums / seq_lengths.astype(token_ratio.dtype)
    owned_mean = jnp.zeros((SEQS,), token_ratio.dtype).at[owners].set(means)
    return (token_ratio, owned_mean)
```

```python
import jax
import jax.numpy as jnp
from jax import lax
from jax.experimental import pallas as pl
from jax.experimental.pallas import tpu as pltpu
from jax.sharding import PartitionSpec as P

MESH = pl.DeviceIdType.MESH
PLANE = 16
NT = (((1,), (1,)), ((), ()))


def head_kernel(x_ref, d_ref, hz_ref, out_ref, xbuf, dbuf, hbuf, stat, lse,
                hsem, xsend, xrecv, dsend, drecv, ssend, srecv, csend, crecv):
    z = lax.axis_index("grp")
    ep = lax.axis_index("ep")
    slot = ep // 2
    core = ep % 2
    zs = lax.axis_size("grp")
    rows = x_ref.shape[0]
    vrows = hz_ref.shape[1]
    cols = 2 * zs

    def plane_peer(j):
        return {"ep": ((slot + j) % PLANE) * 2 + core}

    def col_peer(j):
        other = (z * 2 + core + j) % cols
        return {"grp": other // 2, "ep": slot * 2 + other % 2}

    barrier = pltpu.get_barrier_semaphore()
    for j in range(1, PLANE):
        pl.semaphore_signal(barrier, inc=1, device_id=plane_peer(j), device_id_type=MESH)
    for j in range(1, cols):
        pl.semaphore_signal(barrier, inc=1, device_id=col_peer(j), device_id_type=MESH)
    pl.semaphore_wait(barrier, PLANE - 1 + cols - 1)

    mine = pl.ds(pl.multiple_of(slot * rows, 16), rows)
    xs, ds_ = [], []
    for j in range(1, PLANE):
        cp = pltpu.make_async_remote_copy(
            src_ref=x_ref, dst_ref=xbuf.at[mine, :], send_sem=xsend.at[j], recv_sem=xrecv.at[j],
            device_id=plane_peer(j), device_id_type=MESH)
        cp.start()
        xs.append(cp)
        cd = pltpu.make_async_remote_copy(
            src_ref=d_ref, dst_ref=dbuf.at[mine, :], send_sem=dsend.at[j], recv_sem=drecv.at[j],
            device_id=plane_peer(j), device_id_type=MESH)
        cd.start()
        ds_.append(cd)
    hown = pltpu.make_async_copy(hz_ref, hbuf.at[core], hsem.at[0])
    hown.start()
    hsib = pltpu.make_async_remote_copy(
        src_ref=hz_ref, dst_ref=hbuf.at[core], send_sem=hsem.at[1], recv_sem=hsem.at[2],
        device_id={"ep": slot * 2 + (1 - core)}, device_id_type=MESH)
    hsib.start()
    xown = pltpu.make_async_copy(x_ref, xbuf.at[mine, :], xsend.at[0])
    xown.start()
    down = pltpu.make_async_copy(d_ref, dbuf.at[mine, :], dsend.at[0])
    down.start()
    hown.wait()
    xown.wait()
    down.wait()
    hsib.wait()
    for cp in xs:
        cp.wait()
    for cd in ds_:
        cd.wait()

    stat[slot] = jnp.zeros(stat.shape[1:], jnp.float32)
    lane = lax.broadcasted_iota(jnp.int32, (8, 128), 1)
    weights = jnp.where(lane == 0, 1.0, jnp.where(lane == 1, 64.0, jnp.where(lane == 2, 4096.0, 0.0)))
    weights = weights.astype(jnp.bfloat16)
    tile = 256
    place = lax.broadcasted_iota(jnp.int32, (vrows, tile), 0)

    def tile_body(t, carry):
        rs = pl.ds(pl.multiple_of(t * tile, tile), tile)
        xt = xbuf[rs, :]
        wanted = lax.dot_general(weights, dbuf[rs, :], NT, preferred_element_type=jnp.float32)
        wanted = wanted[0:1, :].astype(jnp.int32)

        def block(b, state):
            m, s, p = state
            logits = lax.dot_general(hbuf[b // zs, b % zs], xt, NT, preferred_element_type=jnp.float32)
            peak = jnp.maximum(m, jnp.max(logits, axis=0, keepdims=True))
            base = ((b % zs) * (2 * PLANE) + slot * 2 + b // zs) * vrows
            total = s * jnp.exp(m - peak) + jnp.sum(jnp.exp(logits - peak), axis=0, keepdims=True)
            hit = place == (wanted - base)
            got = p + jnp.sum(jnp.where(hit, logits, 0.0), axis=0, keepdims=True)
            return (peak, total, got)

        zero = jnp.zeros((1, tile), jnp.float32)
        m, s, p = lax.fori_loop(0, cols, block, (zero - 1e30, zero, zero), unroll=2)
        for k, v in enumerate((m, s, p)):
            both = jnp.concatenate([v[:, :128], v[:, 128:]], axis=0)
            stat[slot, k, pl.ds(t * 2, 2), :] = both
        return carry

    lax.fori_loop(0, PLANE * rows // tile, tile_body, 0)

    ss = []
    for j in range(1, PLANE):
        cp = pltpu.make_async_remote_copy(
            src_ref=stat.at[slot], dst_ref=stat.at[slot], send_sem=ssend.at[j], recv_sem=srecv.at[j],
            device_id=plane_peer(j), device_id_type=MESH)
        cp.start()
        ss.append(cp)
    for cp in ss:
        cp.wait()
    m = stat[0, 0]
    for i in range(1, PLANE):
        m = jnp.maximum(m, stat[i, 0])
    s = jnp.zeros_like(m)
    p = jnp.zeros_like(m)
    for i in range(PLANE):
        s = s + stat[i, 1] * jnp.exp(stat[i, 0] - m)
        p = p + stat[i, 2]
    own = z * 2 + core
    lse[...] = p - (m + jnp.log(s))
    out_ref[own] = lse[...]
    cs = []
    for j in range(1, cols):
        cp = pltpu.make_async_remote_copy(
            src_ref=lse, dst_ref=out_ref.at[own], send_sem=csend.at[j], recv_sem=crecv.at[j],
            device_id=col_peer(j), device_id_type=MESH)
        cp.start()
        cs.append(cp)
    for cp in cs:
        cp.wait()


def head_stage(normed, targets, head_z):
    rows, width = normed.shape
    zs, vrows, _ = head_z.shape
    cols = 2 * zs
    both = jnp.concatenate((targets, targets))
    lane = jnp.arange(128, dtype=jnp.int32)[None, :]
    digit = jnp.where(lane == 0, (both % 64)[:, None],
                      jnp.where(lane == 1, (both // 64 % 64)[:, None],
                                jnp.where(lane == 2, (both // 4096)[:, None], 0)))
    digit = digit.astype(jnp.bfloat16)
    vm = pl.BlockSpec(memory_space=pltpu.VMEM)
    dma = pltpu.SemaphoreType.DMA
    n_pad = 16
    return pl.pallas_call(
        head_kernel,
        out_shape=jax.ShapeDtypeStruct((cols, n_pad, 128), jnp.float32),
        in_specs=[vm, vm, pl.BlockSpec(memory_space=pl.ANY)],
        out_specs=vm,
        scratch_shapes=[
            pltpu.VMEM((PLANE * rows, width), jnp.bfloat16),
            pltpu.VMEM((PLANE * rows, 128), jnp.bfloat16),
            pltpu.VMEM((2, zs, vrows, width), jnp.bfloat16),
            pltpu.VMEM((PLANE, 3, n_pad, 128), jnp.float32),
            pltpu.VMEM((n_pad, 128), jnp.float32),
            dma((3,)), dma((PLANE,)), dma((PLANE,)), dma((PLANE,)), dma((PLANE,)),
            dma((PLANE,)), dma((PLANE,)), dma((cols,)), dma((cols,)),
        ],
        compiler_params=pltpu.CompilerParams(
            collective_id=1, has_side_effects=True, vmem_limit_bytes=60 * 1024 * 1024),
        name="head_stage",
    )(normed, digit, head_z)


def finish(gathered, tok_count, seq_lengths, owners):
    cols = gathered.shape[0]
    zs = cols // 2
    device_index = lax.axis_index(("grp", "ep"))
    z = lax.axis_index("grp")
    ep = lax.axis_index("ep")
    logprob = gathered[:, : PLANE * 2 * tok_count // 128, :].reshape(zs, 2, PLANE, 2, tok_count)
    ratio = logprob[:, :, :, 0] - logprob[:, :, :, 1]
    token_ratio = lax.dynamic_slice(
        ratio, (z, ep % 2, ep // 2, 0), (1, 1, 1, tok_count)).reshape(tok_count)
    offsets = jnp.cumsum(seq_lengths) - seq_lengths
    own = owners == device_index
    first = jnp.sum(jnp.where(own, offsets, 0))
    length = jnp.sum(jnp.where(own, seq_lengths, 0))
    zi = jnp.arange(zs, dtype=jnp.int32)[:, None, None, None]
    ci = jnp.arange(2, dtype=jnp.int32)[None, :, None, None]
    si = jnp.arange(PLANE, dtype=jnp.int32)[None, None, :, None]
    ti = jnp.arange(tok_count, dtype=jnp.int32)[None, None, None, :]
    pos = ((zi * PLANE + si) * 2 + ci) * tok_count + ti
    inside = (pos >= first) & (pos < first + length)
    owned = jnp.sum(jnp.where(inside, ratio, 0.0)) / length.astype(jnp.float32)
    return token_ratio, owned.reshape(1)


def expert_tables(routes, gates, experts, capacity):
    route_hits = routes[:, :, None] == jnp.arange(experts, dtype=jnp.int32)[None, None, :]
    members = jnp.sum(route_hits.astype(jnp.int32), axis=1)
    earlier = jnp.cumsum(members, axis=0) - members
    placed = (members[:, :, None] > 0) & (
        earlier[:, :, None] == jnp.arange(capacity, dtype=jnp.int32)[None, None, :]
    )
    weight = jnp.sum(jnp.where(route_hits, gates[:, :, None], 0.0), axis=1)
    tok_count = routes.shape[0]
    picker = placed.astype(jnp.bfloat16).reshape(tok_count, experts * capacity)
    mixing = (weight[:, :, None] * placed.astype(jnp.float32)).reshape(
        tok_count, experts * capacity
    )
    return (picker, mixing)


def local(
    pol_hidden,
    ref_hidden,
    pol_routes,
    ref_routes,
    pol_gates,
    ref_gates,
    w_gate,
    w_up,
    w_down,
    norm_gain,
    vocab_head,
    targets,
    seq_lengths,
    owners,
):
    groups = lax.axis_size("ep")
    local_experts = w_gate.shape[0]
    experts = local_experts * groups
    tok_count = pol_hidden.shape[0]
    width = pol_hidden.shape[1]
    fanout = pol_routes.shape[1]
    capacity = tok_count * fanout // experts + 2
    pol_pick, pol_mixing = expert_tables(pol_routes, pol_gates, experts, capacity)
    ref_pick, ref_mixing = expert_tables(ref_routes, ref_gates, experts, capacity)
    pol_send = jnp.einsum(
        "ts,td->sd", pol_pick, pol_hidden, preferred_element_type=jnp.float32
    ).astype(jnp.bfloat16)
    ref_send = jnp.einsum(
        "ts,td->sd", ref_pick, ref_hidden, preferred_element_type=jnp.float32
    ).astype(jnp.bfloat16)
    pol_send = pol_send.reshape(groups, local_experts, capacity, width)
    ref_send = ref_send.reshape(groups, local_experts, capacity, width)
    pol_part = lax.all_to_all(pol_send, "ep", split_axis=0, concat_axis=0, tiled=True)
    ref_part = lax.all_to_all(ref_send, "ep", split_axis=0, concat_axis=0, tiled=True)
    slots = pol_part.shape[2]
    joined = jnp.concatenate((pol_part, ref_part), axis=2)
    gate_act = jnp.einsum("nesd,edf->nesf", joined, w_gate, preferred_element_type=jnp.float32)
    up_act = jnp.einsum("nesd,edf->nesf", joined, w_up, preferred_element_type=jnp.float32)
    inner = (jax.nn.silu(gate_act) * up_act).astype(jnp.bfloat16)
    outputs = jnp.einsum(
        "nesf,efd->nesd", inner, w_down, preferred_element_type=jnp.float32
    ).astype(jnp.bfloat16)
    pol_back = lax.all_to_all(outputs[:, :, :slots], "ep", split_axis=0, concat_axis=0, tiled=True)
    ref_back = lax.all_to_all(outputs[:, :, slots:], "ep", split_axis=0, concat_axis=0, tiled=True)

    def mix_back(hidden, mixing, back):
        rows_back = back.reshape(experts * capacity, width).astype(jnp.float32)
        mixed = hidden.astype(jnp.float32) + jnp.dot(
            mixing, rows_back, precision=lax.Precision.HIGHEST
        )
        scale = lax.rsqrt(jnp.mean(mixed * mixed, axis=1, keepdims=True) + 1e-06)
        return (mixed * scale * norm_gain).astype(jnp.bfloat16)

    pol_normed = mix_back(pol_hidden, pol_mixing, pol_back)
    ref_normed = mix_back(ref_hidden, ref_mixing, ref_back)
    normed = jnp.concatenate((pol_normed, ref_normed), axis=0)
    head_z = lax.all_gather(vocab_head, "grp", axis=0)
    gathered = head_stage(normed, targets, head_z)
    return finish(gathered, tok_count, seq_lengths, owners)


def solution(mesh):
    return jax.shard_map(
        local,
        mesh=mesh,
        in_specs=(
            P(("grp", "ep"), None),
            P(("grp", "ep"), None),
            P(("grp", "ep"), None),
            P(("grp", "ep"), None),
            P(("grp", "ep"), None),
            P(("grp", "ep"), None),
            P("ep", None, None),
            P("ep", None, None),
            P("ep", None, None),
            P(),
            P(("grp", "ep"), None),
            P(("grp", "ep")),
            P(),
            P(),
        ),
        out_specs=(P(("grp", "ep")), P(("grp", "ep"))),
        check_vma=False,
    )
```

```python
import jax
import jax.numpy as jnp
from jax import lax
from jax.experimental import pallas as pl
from jax.experimental.pallas import tpu as pltpu
from jax.sharding import PartitionSpec as P

MESH = pl.DeviceIdType.MESH
PLANE = 16
NT = (((1,), (1,)), ((), ()))


def ring_ids(half, d1, d2, piece):
    step = {1: 0, 3: 1, 2: 2 + (piece or 0)}
    inner = step[d1] if d2 == 0 else 4 + d1 * 4 + step[d2]
    return half * 20 + inner


def ring_gather(view, land, near, send_sem, recv_sem, arrived=None):
    sent = []

    def place(half, d1, d2):
        return (d1, d2) if half == 0 else (d2, d1)

    def send(half, d1, d2, piece, second, sign):
        n1, n2 = (d1, (d2 - sign) % 4) if second else ((d1 - sign) % 4, d2)
        k = ring_ids(half, n1, n2, piece)
        axis = (half + second) % 2
        copy = pltpu.make_async_remote_copy(
            src_ref=view(*place(half, d1, d2), half, piece),
            dst_ref=land(*place(half, d1, d2), *place(half, n1, n2), half, piece),
            send_sem=send_sem.at[k], recv_sem=recv_sem.at[k],
            device_id=near(axis, sign), device_id_type=MESH)
        copy.start()
        sent.append(copy)

    def wait(half, d1, d2, piece=None):
        k = ring_ids(half, d1, d2, piece)
        ref = view(*place(half, d1, d2), half, piece)
        pltpu.make_async_remote_copy(
            src_ref=ref, dst_ref=ref, send_sem=send_sem.at[k], recv_sem=recv_sem.at[k],
            device_id=near(0, 1), device_id_type=MESH).wait_recv()

    def full(half, d1, d2):
        if arrived is not None:
            arrived(*place(half, d1, d2), half)

    halves = (0, 1)
    for half in halves:
        send(half, 0, 0, None, 0, 1)
        send(half, 0, 0, None, 0, -1)
    for half in halves:
        send(half, 0, 0, None, 1, 1)
        send(half, 0, 0, None, 1, -1)
        full(half, 0, 0)
    for d1, sign, piece in ((3, 1, 0), (1, -1, 1)):
        for half in halves:
            wait(half, d1, 0)
            send(half, d1, 0, piece, 0, sign)
            send(half, d1, 0, None, 1, 1)
            send(half, d1, 0, None, 1, -1)
            full(half, d1, 0)

    def relay(d1):
        for d2, sign, piece in ((3, 1, 0), (1, -1, 1)):
            for half in halves:
                wait(half, d1, d2)
                send(half, d1, d2, piece, 1, sign)
                full(half, d1, d2)

    relay(0)
    for half in halves:
        wait(half, 2, 0, 0)
        wait(half, 2, 0, 1)
        send(half, 2, 0, None, 1, 1)
        send(half, 2, 0, None, 1, -1)
        full(half, 2, 0)
    for d1 in (3, 1, 2):
        relay(d1)
    for d1 in range(4):
        for half in halves:
            wait(half, d1, 2, 0)
            wait(half, d1, 2, 1)
            full(half, d1, 2)
    return sent


def torus(ep):
    slot = ep // 2
    core = ep % 2
    y = slot // 4
    x = slot % 4

    def at(dx, dy, c):
        return {"ep": (((y + dy) % 4) * 4 + (x + dx) % 4) * 2 + c}

    def near(axis, sign):
        return at(sign, 0, core) if axis == 0 else at(0, sign, core)

    return slot, core, y, x, at, near


def expert_kernel(ph_ref, rh_ref, pr_ref, rr_ref, pg_ref, rg_ref, wg_hbm, wu_hbm, wd_hbm, gain_ref,
                  out_ref, buf, obuf, back, gmat, wg, wu, wd,
                  lsem, wsem, asend, arecv, bsend, brecv, osend, orecv):
    ep = lax.axis_index("ep")
    slot, core, y, x, at, near = torus(ep)
    toks = ph_ref.shape[0]
    rows = 2 * toks
    pad = buf.shape[2] - rows
    width = ph_ref.shape[1]
    f32, bf16 = jnp.float32, jnp.bfloat16
    half_w = width // 2
    quarter = width // 4

    loads = [pltpu.make_async_copy(src, dst, wsem.at[i])
             for i, (src, dst) in enumerate(((wg_hbm, wg), (wu_hbm, wu), (wd_hbm, wd)))]
    for cp in loads:
        cp.start()
    barrier = pltpu.get_barrier_semaphore()
    for r in range(PLANE):
        for c in range(2):
            if r == 0 and c == 1:
                continue
            cc = 1 - core if r == 0 else c
            pl.semaphore_signal(barrier, inc=1, device_id=at(r % 4, r // 4, cc), device_id_type=MESH)
    buf[0, core, pl.ds(0, toks), :] = ph_ref[...]
    buf[0, core, pl.ds(toks, toks), :] = rh_ref[...]

    lane = lax.broadcasted_iota(jnp.int32, (toks, 128), 1)
    token = lax.broadcasted_iota(jnp.int32, (toks, 128), 0).astype(f32)
    lower = (lax.broadcasted_iota(jnp.int32, (toks, toks), 0)
             > lax.broadcasted_iota(jnp.int32, (toks, toks), 1)).astype(bf16)
    ranks, mass, tab = [], [], []
    for model, (routes, gates) in enumerate(((pr_ref, pg_ref), (rr_ref, rg_ref))):
        member = jnp.zeros((toks, 128), f32)
        weight = jnp.zeros((toks, 128), f32)
        for k in range(routes.shape[1]):
            match = routes[:, k:k + 1] == lane
            member = member + jnp.where(match, 1.0, 0.0)
            weight = weight + jnp.where(match, gates[:, k:k + 1], 0.0)
        earlier = jnp.dot(lower, member.astype(bf16), preferred_element_type=f32)
        rank = jnp.where(member > 0.0, earlier, -1.0)
        for s in range(8):
            hit = rank == float(s)
            found = jnp.sum(jnp.where(hit, token + float(model * toks) - 128.0, 0.0), axis=0, keepdims=True)
            tab.append(found + 128.0)
        ranks.append(rank)
        mass.append(weight)
    for r in range(PLANE):
        for c in range(2):
            buf[r, c, pl.ds(rows, pad), pl.ds(half_w, half_w)] = jnp.zeros((pad, half_w), bf16)
    table = jnp.concatenate(tab, axis=0).astype(bf16)
    buf[0, core, pl.ds(rows, pad), pl.ds(0, 128)] = table
    buf[0, core, pl.ds(rows, pad), pl.ds(128, half_w - 128)] = jnp.zeros((pad, half_w - 128), bf16)
    pl.semaphore_wait(barrier, 2 * PLANE - 1)

    def piece_view(dx, dy, half, piece):
        height = rows + pad if half == 0 else rows
        start = half * half_w + (piece or 0) * quarter
        size = half_w if piece is None else quarter
        return buf.at[dy * 4 + dx, core, pl.ds(0, height), pl.ds(start, size)]

    def land(dx, dy, nx, ny, half, piece):
        return piece_view(nx, ny, half, piece)

    across = []

    def arrived(dx, dy, half):
        k = (dy * 4 + dx) * 2 + half
        ref = piece_view(dx, dy, half, None)
        cp = pltpu.make_async_remote_copy(
            src_ref=ref, dst_ref=ref, send_sem=bsend.at[k], recv_sem=brecv.at[k],
            device_id=at(0, 0, 1 - core), device_id_type=MESH)
        cp.start()
        across.append((dx, dy, half, k, cp))

    sent = ring_gather(piece_view, land, near, asend, arecv, arrived)

    lanes = 2 * PLANE * 32
    spread = (lax.broadcasted_iota(jnp.int32, (128, lanes), 1) // 16
              == lax.broadcasted_iota(jnp.int32, (128, lanes), 0)).astype(bf16)
    col = lax.broadcasted_iota(jnp.int32, (toks, lanes), 1)
    for model in range(2):
        hi = mass[model].astype(bf16)
        lo = (mass[model] - hi.astype(f32)).astype(bf16)
        rank = jnp.dot(ranks[model].astype(bf16), spread, preferred_element_type=f32)
        fits = (rank == (col % 8).astype(f32)) & ((col // 8) % 2 == model)
        for part, value in enumerate((hi, lo)):
            wide = jnp.dot(value, spread, preferred_element_type=f32)
            gmat[pl.ds(part * rows + model * toks, toks), :] = jnp.where(fits, wide, 0.0)

    for dx, dy, half, k, cp in across:
        height = rows + pad if half == 0 else rows
        ref = buf.at[dy * 4 + dx, 1 - core, pl.ds(0, height), pl.ds(half * half_w, half_w)]
        pltpu.make_async_remote_copy(
            src_ref=ref, dst_ref=ref, send_sem=bsend.at[k], recv_sem=brecv.at[k],
            device_id=at(0, 0, 1 - core), device_id_type=MESH).wait_recv()
    for cp in loads:
        cp.wait()

    height = rows + pad
    span = PLANE // 2
    count = span * 2 * 16
    deep = span * 2 * height
    sel_lane = lax.broadcasted_iota(jnp.int32, (count, deep), 1)
    tab_lane = lax.broadcasted_iota(jnp.int32, (count, 128), 1)
    block_row = lax.broadcasted_iota(jnp.int32, (count, 1), 0) // 16
    returns = []
    for g in range(2):
        tokens = buf[g * span:(g + 1) * span].reshape(deep, width)
        tabs = buf[g * span:(g + 1) * span, :, rows:rows + pad, 0:128].reshape(count, 128).astype(f32)
        for e in range(2):
            at_e = jnp.sum(jnp.where(tab_lane == ep * 2 + e, tabs, 0.0), axis=1, keepdims=True).astype(jnp.int32)
            index = jnp.where(at_e < 128, at_e + block_row * height, -1)
            pick = (index == sel_lane).astype(bf16)
            taken = jnp.dot(pick, tokens, preferred_element_type=f32).astype(bf16)
            gate = jnp.dot(taken, wg[e], preferred_element_type=f32)
            up = jnp.dot(taken, wu[e], preferred_element_type=f32)
            inner = (gate / (1.0 + jnp.exp(-gate)) * up).astype(bf16)
            out = jnp.dot(inner, wd[e], preferred_element_type=f32).astype(bf16)
            obuf[g * span:(g + 1) * span, :, e * 16:(e + 1) * 16, :] = out.reshape(span, 2, 16, width)
        for r in range(g * span, (g + 1) * span):
            for c in range(2):
                if r == 0:
                    if c == 1:
                        continue
                    cc = 1 - core
                else:
                    cc = c
                cp = pltpu.make_async_remote_copy(
                    src_ref=obuf.at[r, cc], dst_ref=back.at[ep],
                    send_sem=osend.at[r * 2 + c], recv_sem=orecv.at[r * 2 + core],
                    device_id=at(r % 4, r // 4, cc), device_id_type=MESH)
                cp.start()
                returns.append(cp)
    back[ep] = obuf[0, core]
    for r in range(PLANE):
        for c in range(2):
            if r == 0:
                if c == 1:
                    continue
                cc = 1 - core
            else:
                cc = c
            source = at(-(r % 4), -(r // 4), cc)["ep"]
            pltpu.make_async_remote_copy(
                src_ref=back.at[source], dst_ref=back.at[source],
                send_sem=osend.at[r * 2 + c], recv_sem=orecv.at[r * 2 + cc],
                device_id=at(0, 0, 1 - core), device_id_type=MESH).wait_recv()
    parts = jnp.dot(gmat[...].astype(bf16), back[...].reshape(lanes, width), preferred_element_type=f32)
    for model, hidden in enumerate((ph_ref, rh_ref)):
        base = model * toks
        mixed = hidden[...].astype(f32) + (parts[base:base + toks] + parts[rows + base:rows + base + toks])
        scale = lax.rsqrt(jnp.mean(mixed * mixed, axis=1, keepdims=True) + 1e-06)
        out_ref[pl.ds(base, toks), :] = (mixed * scale * gain_ref[...]).astype(bf16)
    for cp in sent:
        cp.wait_send()
    for item in across:
        item[4].wait_send()
    for cp in returns:
        cp.wait_send()


def expert_stage(pol_hidden, ref_hidden, pol_routes, ref_routes, pol_gates, ref_gates, w_gate, w_up, w_down, norm_gain):
    toks, width = pol_hidden.shape
    ff = w_gate.shape[2]
    vm = pl.BlockSpec(memory_space=pltpu.VMEM)
    hbm = pl.BlockSpec(memory_space=pl.ANY)
    dma = pltpu.SemaphoreType.DMA
    bf16 = jnp.bfloat16
    return pl.pallas_call(
        expert_kernel,
        out_shape=jax.ShapeDtypeStruct((2 * toks, width), bf16),
        in_specs=[vm] * 6 + [hbm] * 3 + [vm],
        out_specs=vm,
        scratch_shapes=[
            pltpu.VMEM((PLANE, 2, 2 * toks + 16, width), bf16),
            pltpu.VMEM((PLANE, 2, 32, width), bf16),
            pltpu.VMEM((2 * PLANE, 32, width), bf16),
            pltpu.VMEM((4 * toks, 2 * PLANE * 32), jnp.float32),
            pltpu.VMEM((2, width, ff), bf16),
            pltpu.VMEM((2, width, ff), bf16),
            pltpu.VMEM((2, ff, width), bf16),
            dma((2,)), dma((3,)), dma((40,)), dma((40,)), dma((32,)), dma((32,)), dma((32,)), dma((32,)),
        ],
        compiler_params=pltpu.CompilerParams(
            collective_id=2, has_side_effects=True, vmem_limit_bytes=60 * 1024 * 1024),
        name="expert_stage",
    )(pol_hidden, ref_hidden, pol_routes, ref_routes, pol_gates, ref_gates, w_gate, w_up, w_down,
      norm_gain.reshape(1, width))


def head_kernel(x_ref, hz_ref, out_ref, xbuf, hbuf, stat, lse,
                hsem, xsend, xrecv, ssend, srecv, csend, crecv):
    z = lax.axis_index("grp")
    ep = lax.axis_index("ep")
    slot, core, y, x, at, near = torus(ep)
    zs = lax.axis_size("grp")
    rows = x_ref.shape[0]
    vrows = hz_ref.shape[1]
    cols = 2 * zs

    def plane_peer(j):
        return {"ep": ((slot + j) % PLANE) * 2 + core}

    def col_peer(j):
        other = (z * 2 + core + j) % cols
        return {"grp": other // 2, "ep": slot * 2 + other % 2}

    barrier = pltpu.get_barrier_semaphore()
    for j in range(1, PLANE):
        pl.semaphore_signal(barrier, inc=1, device_id=plane_peer(j), device_id_type=MESH)
    for j in range(1, cols):
        pl.semaphore_signal(barrier, inc=1, device_id=col_peer(j), device_id_type=MESH)
    xbuf[pl.ds(pl.multiple_of(slot * rows, 16), rows), :] = x_ref[...]
    pl.semaphore_wait(barrier, PLANE - 1 + cols - 1)

    width = x_ref.shape[1]

    def view(dx, dy, half, piece):
        where = ((y + dy) % 4) * 4 + (x + dx) % 4
        start, size = ((0, 512), (512, width - 512))[half]
        if piece is not None:
            start, size = ((start, 256), (start + 256, size - 256))[piece]
        return xbuf.at[pl.ds(pl.multiple_of(where * rows, 16), rows), pl.ds(start, size)]

    def land(dx, dy, nx, ny, half, piece):
        return view(dx, dy, half, piece)

    hown = pltpu.make_async_copy(hz_ref, hbuf.at[core], hsem.at[0])
    hown.start()
    hsib = pltpu.make_async_remote_copy(
        src_ref=hz_ref, dst_ref=hbuf.at[core], send_sem=hsem.at[1], recv_sem=hsem.at[2],
        device_id={"ep": slot * 2 + (1 - core)}, device_id_type=MESH)
    hsib.start()
    sent = ring_gather(view, land, near, xsend, xrecv)
    hown.wait()
    hsib.wait()

    stat[slot] = jnp.zeros(stat.shape[1:], jnp.float32)
    lane = lax.broadcasted_iota(jnp.int32, (8, 128), 1)
    weights = jnp.where(lane == 0, 1.0, jnp.where(lane == 1, 64.0, jnp.where(lane == 2, 4096.0, 0.0)))
    weights = weights.astype(jnp.bfloat16)
    tile = 256
    place = lax.broadcasted_iota(jnp.int32, (vrows, tile), 0)

    def tile_body(t, carry):
        rs = pl.ds(pl.multiple_of(t * tile, tile), tile)
        xt = xbuf[rs, pl.ds(0, width - 128)]
        wanted = lax.dot_general(weights, xbuf[rs, pl.ds(width - 128, 128)], NT, preferred_element_type=jnp.float32)
        wanted = wanted[0:1, :].astype(jnp.int32)

        def block(b, state):
            m, s, p = state
            logits = lax.dot_general(hbuf[b // zs, b % zs], xt, NT, preferred_element_type=jnp.float32)
            peak = jnp.maximum(m, jnp.max(logits, axis=0, keepdims=True))
            base = ((b % zs) * (2 * PLANE) + slot * 2 + b // zs) * vrows
            total = s * jnp.exp(m - peak) + jnp.sum(jnp.exp(logits - peak), axis=0, keepdims=True)
            hit = place == (wanted - base)
            got = p + jnp.sum(jnp.where(hit, logits, 0.0), axis=0, keepdims=True)
            return (peak, total, got)

        zero = jnp.zeros((1, tile), jnp.float32)
        m, s, p = lax.fori_loop(0, cols, block, (zero - 1e30, zero, zero), unroll=2)
        for k, v in enumerate((m, s, p)):
            both = jnp.concatenate([v[:, :128], v[:, 128:]], axis=0)
            stat[slot, k, pl.ds(t * 2, 2), :] = both
        return carry

    lax.fori_loop(0, PLANE * rows // tile, tile_body, 0)

    ss = []
    for j in range(1, PLANE):
        cp = pltpu.make_async_remote_copy(
            src_ref=stat.at[slot], dst_ref=stat.at[slot], send_sem=ssend.at[j], recv_sem=srecv.at[j],
            device_id=plane_peer(j), device_id_type=MESH)
        cp.start()
        ss.append(cp)
    for cp in ss:
        cp.wait()
    m = stat[0, 0]
    for i in range(1, PLANE):
        m = jnp.maximum(m, stat[i, 0])
    s = jnp.zeros_like(m)
    p = jnp.zeros_like(m)
    for i in range(PLANE):
        s = s + stat[i, 1] * jnp.exp(stat[i, 0] - m)
        p = p + stat[i, 2]
    own = z * 2 + core
    lse[...] = p - (m + jnp.log(s))
    out_ref[own] = lse[...]
    cs = []
    for j in range(1, cols):
        cp = pltpu.make_async_remote_copy(
            src_ref=lse, dst_ref=out_ref.at[own], send_sem=csend.at[j], recv_sem=crecv.at[j],
            device_id=col_peer(j), device_id_type=MESH)
        cp.start()
        cs.append(cp)
    for cp in cs:
        cp.wait()
    for cp in sent:
        cp.wait_send()


def head_stage(normed, targets, head_z):
    rows, width = normed.shape
    zs, vrows, _ = head_z.shape
    cols = 2 * zs
    both = jnp.concatenate((targets, targets))
    lane = jnp.arange(128, dtype=jnp.int32)[None, :]
    digit = jnp.where(lane == 0, (both % 64)[:, None],
                      jnp.where(lane == 1, (both // 64 % 64)[:, None],
                                jnp.where(lane == 2, (both // 4096)[:, None], 0)))
    digit = digit.astype(jnp.bfloat16)
    vm = pl.BlockSpec(memory_space=pltpu.VMEM)
    dma = pltpu.SemaphoreType.DMA
    n_pad = 16
    return pl.pallas_call(
        head_kernel,
        out_shape=jax.ShapeDtypeStruct((cols, n_pad, 128), jnp.float32),
        in_specs=[vm, pl.BlockSpec(memory_space=pl.ANY)],
        out_specs=vm,
        scratch_shapes=[
            pltpu.VMEM((PLANE * rows, width + 128), jnp.bfloat16),
            pltpu.VMEM((2, zs, vrows, width), jnp.bfloat16),
            pltpu.VMEM((PLANE, 3, n_pad, 128), jnp.float32),
            pltpu.VMEM((n_pad, 128), jnp.float32),
            dma((3,)), dma((40,)), dma((40,)),
            dma((PLANE,)), dma((PLANE,)), dma((cols,)), dma((cols,)),
        ],
        compiler_params=pltpu.CompilerParams(
            collective_id=1, has_side_effects=True, vmem_limit_bytes=60 * 1024 * 1024),
        name="head_stage",
    )(jnp.concatenate((normed, digit), axis=1), head_z)


def finish(gathered, tok_count, seq_lengths, owners):
    cols = gathered.shape[0]
    zs = cols // 2
    device_index = lax.axis_index(("grp", "ep"))
    z = lax.axis_index("grp")
    ep = lax.axis_index("ep")
    logprob = gathered[:, : PLANE * 2 * tok_count // 128, :].reshape(zs, 2, PLANE, 2, tok_count)
    ratio = logprob[:, :, :, 0] - logprob[:, :, :, 1]
    token_ratio = lax.dynamic_slice(
        ratio, (z, ep % 2, ep // 2, 0), (1, 1, 1, tok_count)).reshape(tok_count)
    offsets = jnp.cumsum(seq_lengths) - seq_lengths
    own = owners == device_index
    first = jnp.sum(jnp.where(own, offsets, 0))
    length = jnp.sum(jnp.where(own, seq_lengths, 0))
    zi = jnp.arange(zs, dtype=jnp.int32)[:, None, None, None]
    ci = jnp.arange(2, dtype=jnp.int32)[None, :, None, None]
    si = jnp.arange(PLANE, dtype=jnp.int32)[None, None, :, None]
    ti = jnp.arange(tok_count, dtype=jnp.int32)[None, None, None, :]
    pos = ((zi * PLANE + si) * 2 + ci) * tok_count + ti
    inside = (pos >= first) & (pos < first + length)
    owned = jnp.sum(jnp.where(inside, ratio, 0.0)) / length.astype(jnp.float32)
    return token_ratio, owned.reshape(1)


def local(
    pol_hidden,
    ref_hidden,
    pol_routes,
    ref_routes,
    pol_gates,
    ref_gates,
    w_gate,
    w_up,
    w_down,
    norm_gain,
    vocab_head,
    targets,
    seq_lengths,
    owners,
):
    tok_count = pol_hidden.shape[0]
    normed = expert_stage(pol_hidden, ref_hidden, pol_routes, ref_routes, pol_gates, ref_gates,
                          w_gate, w_up, w_down, norm_gain)
    head_z = lax.all_gather(vocab_head, "grp", axis=0)
    gathered = head_stage(normed, targets, head_z)
    return finish(gathered, tok_count, seq_lengths, owners)


def solution(mesh):
    return jax.shard_map(
        local,
        mesh=mesh,
        in_specs=(
            P(("grp", "ep"), None),
            P(("grp", "ep"), None),
            P(("grp", "ep"), None),
            P(("grp", "ep"), None),
            P(("grp", "ep"), None),
            P(("grp", "ep"), None),
            P("ep", None, None),
            P("ep", None, None),
            P("ep", None, None),
            P(),
            P(("grp", "ep"), None),
            P(("grp", "ep")),
            P(),
            P(),
        ),
        out_specs=(P(("grp", "ep")), P(("grp", "ep"))),
        check_vma=False,
    )
```

```python
import jax
import jax.numpy as jnp
from jax import lax
from jax.experimental import pallas as pl
from jax.experimental.pallas import tpu as pltpu
from jax.sharding import PartitionSpec as P

MESH = pl.DeviceIdType.MESH
PLANE = 16
NT = (((1,), (1,)), ((), ()))


def ring_ids(half, d1, d2, piece):
    step = {1: 0, 3: 1, 2: 2 + (piece or 0)}
    inner = step[d1] if d2 == 0 else 4 + d1 * 4 + step[d2]
    return half * 20 + inner


def ring_gather(view, land, near, send_sem, recv_sem, arrived=None, midway=None):
    sent = []

    def place(half, d1, d2):
        return (d1, d2) if half == 0 else (d2, d1)

    def send(half, d1, d2, piece, second, sign):
        n1, n2 = (d1, (d2 - sign) % 4) if second else ((d1 - sign) % 4, d2)
        k = ring_ids(half, n1, n2, piece)
        axis = (half + second) % 2
        copy = pltpu.make_async_remote_copy(
            src_ref=view(*place(half, d1, d2), half, piece),
            dst_ref=land(*place(half, d1, d2), *place(half, n1, n2), half, piece),
            send_sem=send_sem.at[k], recv_sem=recv_sem.at[k],
            device_id=near(axis, sign), device_id_type=MESH)
        copy.start()
        sent.append(copy)

    def wait(half, d1, d2, piece=None):
        k = ring_ids(half, d1, d2, piece)
        ref = view(*place(half, d1, d2), half, piece)
        pltpu.make_async_remote_copy(
            src_ref=ref, dst_ref=ref, send_sem=send_sem.at[k], recv_sem=recv_sem.at[k],
            device_id=near(0, 1), device_id_type=MESH).wait_recv()

    def full(half, d1, d2):
        if arrived is not None:
            arrived(*place(half, d1, d2), half)

    halves = (0, 1)
    for half in halves:
        send(half, 0, 0, None, 0, 1)
        send(half, 0, 0, None, 0, -1)
    for half in halves:
        send(half, 0, 0, None, 1, 1)
        send(half, 0, 0, None, 1, -1)
        full(half, 0, 0)
    for d1, sign, piece in ((3, 1, 0), (1, -1, 1)):
        for half in halves:
            wait(half, d1, 0)
            send(half, d1, 0, piece, 0, sign)
            send(half, d1, 0, None, 1, 1)
            send(half, d1, 0, None, 1, -1)
            full(half, d1, 0)

    def relay(d1):
        for d2, sign, piece in ((3, 1, 0), (1, -1, 1)):
            for half in halves:
                wait(half, d1, d2)
                send(half, d1, d2, piece, 1, sign)
                full(half, d1, d2)

    relay(0)
    if midway is not None:
        midway()
    for half in halves:
        wait(half, 2, 0, 0)
        wait(half, 2, 0, 1)
        send(half, 2, 0, None, 1, 1)
        send(half, 2, 0, None, 1, -1)
        full(half, 2, 0)
    for d1 in (3, 1, 2):
        relay(d1)
    for d1 in range(4):
        for half in halves:
            wait(half, d1, 2, 0)
            wait(half, d1, 2, 1)
            full(half, d1, 2)
    return sent


def torus(ep):
    slot = ep // 2
    core = ep % 2
    y = slot // 4
    x = slot % 4

    def at(dx, dy, c):
        return {"ep": (((y + dy) % 4) * 4 + (x + dx) % 4) * 2 + c}

    def near(axis, sign):
        return at(sign, 0, core) if axis == 0 else at(0, sign, core)

    return slot, core, y, x, at, near


def kernel(ph_ref, rh_ref, pr_ref, rr_ref, pg_ref, rg_ref, wg_hbm, wu_hbm, wd_hbm, gain_ref,
           head_hbm, tgt_ref, len_ref, own_ref, out_ref,
           buf, obuf, back, gmat, wg, wu, wd, xbuf, hbuf, stat, share, gath,
           wsem, asend, arecv, bsend, brecv, osend, orecv, zsend, zrecv, csend, crecv,
           xsend, xrecv, ssend, srecv, fsend, frecv):
    z = lax.axis_index("grp")
    ep = lax.axis_index("ep")
    zs = lax.axis_size("grp")
    slot, core, y, x, at, near = torus(ep)
    toks = ph_ref.shape[0]
    rows = 2 * toks
    pad = buf.shape[2] - rows
    height = rows + pad
    width = ph_ref.shape[1]
    vrows = head_hbm.shape[0]
    cols = 2 * zs
    f32, bf16 = jnp.float32, jnp.bfloat16
    half_w = width // 2
    quarter = width // 4

    def col_peer(j):
        other = (z * 2 + core + j) % cols
        return {"grp": other // 2, "ep": slot * 2 + other % 2}

    loads = [pltpu.make_async_copy(src, dst, wsem.at[i])
             for i, (src, dst) in enumerate(((wg_hbm, wg), (wu_hbm, wu), (wd_hbm, wd), (head_hbm, hbuf.at[core, z])))]
    for cp in loads:
        cp.start()
    barrier = pltpu.get_barrier_semaphore()
    pairs = [(r, c) for r in range(PLANE) for c in range(2) if (r, c) != (0, 1)]

    def pair(r, c):
        cc = 1 - core if r == 0 else c
        return at(r % 4, r // 4, cc), cc

    for r, c in pairs:
        pl.semaphore_signal(barrier, inc=1, device_id=pair(r, c)[0], device_id_type=MESH)
    for dz in range(1, zs):
        for c in range(2):
            pl.semaphore_signal(barrier, inc=1, device_id={"grp": (z + dz) % zs, "ep": slot * 2 + c},
                                device_id_type=MESH)
    buf[0, core, pl.ds(0, toks), :] = ph_ref[...]
    buf[0, core, pl.ds(toks, toks), :] = rh_ref[...]

    lane = lax.broadcasted_iota(jnp.int32, (toks, 128), 1).astype(f32)
    token = lax.broadcasted_iota(jnp.int32, (toks, 128), 0).astype(f32)
    at_row = lax.broadcasted_iota(jnp.int32, (toks, toks), 0)
    at_col = lax.broadcasted_iota(jnp.int32, (toks, toks), 1)
    lower = (at_row > at_col).astype(bf16)
    same = (at_row == at_col).astype(bf16)
    ranks, mass, tab = [], [], []
    for model, (routes, gates) in enumerate(((pr_ref, pg_ref), (rr_ref, rg_ref))):
        wide = gates[...]
        high = wide.astype(bf16)
        low = (wide - high.astype(f32)).astype(bf16)
        turn = [lax.dot_general(same, v, NT, preferred_element_type=f32)
                for v in (routes[...].astype(f32).astype(bf16), high, low)]
        member = jnp.zeros((toks, 128), f32)
        parts = [member, member]
        for k in range(routes.shape[0]):
            match = turn[0][:, k:k + 1] == lane
            member = member + jnp.where(match, 1.0, 0.0)
            parts = [v + jnp.where(match, t[:, k:k + 1], 0.0) for v, t in zip(parts, turn[1:])]
        earlier = jnp.dot(lower, member.astype(bf16), preferred_element_type=f32)
        rank = jnp.where(member > 0.0, earlier, -1.0)
        for s in range(8):
            hit = rank == float(s)
            found = jnp.sum(jnp.where(hit, token + float(model * toks) - 128.0, 0.0), axis=0, keepdims=True)
            tab.append(found + 128.0)
        ranks.append(rank.astype(bf16))
        mass.append([v.astype(bf16) for v in parts])
    for r in range(PLANE):
        for c in range(2):
            buf[r, c, pl.ds(rows, pad), pl.ds(half_w, half_w)] = jnp.zeros((pad, half_w), bf16)
    table = jnp.concatenate(tab, axis=0).astype(bf16)
    buf[0, core, pl.ds(rows, pad), pl.ds(0, 128)] = table
    buf[0, core, pl.ds(rows, pad), pl.ds(128, half_w - 128)] = jnp.zeros((pad, half_w - 128), bf16)
    pl.semaphore_wait(barrier, len(pairs) + 2 * (zs - 1))

    ring = []

    def z_piece(block, part):
        where = hbuf.at[core, (z + block) % zs]
        if part is None:
            return where
        return where.at[:, pl.ds(part * half_w, half_w)]

    def z_send(block, sign, step):
        part = None if step < 3 else (0 if sign > 0 else 1)
        k = step * 2 + (0 if sign > 0 else 1)
        ref = z_piece(block, part)
        cp = pltpu.make_async_remote_copy(
            src_ref=head_hbm if step == 0 else ref, dst_ref=ref, send_sem=zsend.at[k], recv_sem=zrecv.at[k],
            device_id={"grp": (z + sign) % zs}, device_id_type=MESH)
        cp.start()
        ring.append(cp)

    def z_wait(block, sign, step):
        part = None if step < 3 else (0 if sign > 0 else 1)
        k = step * 2 + (0 if sign > 0 else 1)
        ref = z_piece(block, part)
        pltpu.make_async_remote_copy(
            src_ref=ref, dst_ref=ref, send_sem=zsend.at[k], recv_sem=zrecv.at[k],
            device_id={"grp": (z + sign) % zs}, device_id_type=MESH).wait_recv()

    def cross(block, k, source=None):
        ref = hbuf.at[core, (z + block) % zs]
        cp = pltpu.make_async_remote_copy(
            src_ref=ref if source is None else source, dst_ref=ref, send_sem=csend.at[k], recv_sem=crecv.at[k],
            device_id=at(0, 0, 1 - core), device_id_type=MESH)
        cp.start()
        ring.append(cp)

    def pump(step):
        for sign in (1, -1):
            z_wait(-sign * (step + 1), sign, step)
            z_send(-sign * (step + 1), sign, step + 1)
        for i, sign in enumerate((1, -1)):
            cross(-sign * (step + 1), 1 + step * 2 + i)

    def last_pump():
        for sign in (1, -1):
            z_wait(-sign * 4, sign, 3)
        cross(4, 7)

    z_send(0, 1, 0)
    z_send(0, -1, 0)

    def piece_view(dx, dy, half, piece):
        start = half * half_w + (piece or 0) * quarter
        size = half_w if piece is None else quarter
        return buf.at[dy * 4 + dx, core, pl.ds(0, height if half == 0 else rows), pl.ds(start, size)]

    def land(dx, dy, nx, ny, half, piece):
        return piece_view(nx, ny, half, piece)

    across = []

    def arrived(dx, dy, half):
        k = (dy * 4 + dx) * 2 + half
        ref = piece_view(dx, dy, half, None)
        cp = pltpu.make_async_remote_copy(
            src_ref=ref, dst_ref=ref, send_sem=bsend.at[k], recv_sem=brecv.at[k],
            device_id=at(0, 0, 1 - core), device_id_type=MESH)
        cp.start()
        across.append((dx, dy, half, k, cp))

    sent = ring_gather(piece_view, land, near, asend, arecv, arrived, lambda: pump(0))
    cross(0, 0, head_hbm)

    lanes = 2 * PLANE * 32
    spread = (lax.broadcasted_iota(jnp.int32, (128, lanes), 1) // 16
              == lax.broadcasted_iota(jnp.int32, (128, lanes), 0)).astype(bf16)
    col = lax.broadcasted_iota(jnp.int32, (toks, lanes), 1)
    for model in range(2):
        rank = jnp.dot(ranks[model], spread, preferred_element_type=f32)
        fits = (rank == (col % 8).astype(f32)) & ((col // 8) % 2 == model)
        for part, value in enumerate(mass[model]):
            wide = jnp.dot(value, spread, preferred_element_type=f32)
            gmat[pl.ds(part * rows + model * toks, toks), :] = jnp.where(fits, wide, 0.0)

    for dx, dy, half, k, cp in across:
        ref = buf.at[dy * 4 + dx, 1 - core, pl.ds(0, height if half == 0 else rows), pl.ds(half * half_w, half_w)]
        pltpu.make_async_remote_copy(
            src_ref=ref, dst_ref=ref, send_sem=bsend.at[k], recv_sem=brecv.at[k],
            device_id=at(0, 0, 1 - core), device_id_type=MESH).wait_recv()
    for cp in loads:
        cp.wait()

    span = PLANE // 2
    count = span * 2 * 16
    deep = span * 2 * height
    sel_lane = lax.broadcasted_iota(jnp.int32, (count, deep), 1)
    tab_lane = lax.broadcasted_iota(jnp.int32, (count, 128), 1)
    block_row = lax.broadcasted_iota(jnp.int32, (count, 1), 0) // 16
    returns = []
    for g in range(2):
        tokens = buf[g * span:(g + 1) * span].reshape(deep, width)
        tabs = buf[g * span:(g + 1) * span, :, rows:rows + pad, 0:128].reshape(count, 128).astype(f32)
        for e in range(2):
            at_e = jnp.sum(jnp.where(tab_lane == ep * 2 + e, tabs, 0.0), axis=1, keepdims=True).astype(jnp.int32)
            index = jnp.where(at_e < 128, at_e + block_row * height, -1)
            pick = (index == sel_lane).astype(bf16)
            taken = jnp.dot(pick, tokens, preferred_element_type=f32).astype(bf16)
            gate = jnp.dot(taken, wg[e], preferred_element_type=f32)
            up = jnp.dot(taken, wu[e], preferred_element_type=f32)
            inner = (gate / (1.0 + jnp.exp(-gate)) * up).astype(bf16)
            out = jnp.dot(inner, wd[e], preferred_element_type=f32).astype(bf16)
            obuf[g * span:(g + 1) * span, :, e * 16:(e + 1) * 16, :] = out.reshape(span, 2, 16, width)
        for r, c in pairs:
            if r // span != g:
                continue
            dev, cc = pair(r, c)
            cp = pltpu.make_async_remote_copy(
                src_ref=obuf.at[r, cc], dst_ref=back.at[ep],
                send_sem=osend.at[r * 2 + c], recv_sem=orecv.at[r * 2 + core],
                device_id=dev, device_id_type=MESH)
            cp.start()
            returns.append(cp)
        if g == 0:
            pump(1)
    back[ep] = obuf[0, core]
    pump(2)
    for r, c in pairs:
        cc = 1 - core if r == 0 else c
        source = at(-(r % 4), -(r // 4), cc)["ep"]
        pltpu.make_async_remote_copy(
            src_ref=back.at[source], dst_ref=back.at[source],
            send_sem=osend.at[r * 2 + c], recv_sem=orecv.at[r * 2 + cc],
            device_id=at(0, 0, 1 - core), device_id_type=MESH).wait_recv()
    mixing = jnp.dot(gmat[...].astype(bf16), back[...].reshape(lanes, width), preferred_element_type=f32)
    here = pl.multiple_of(slot * rows, 16)
    normed = []
    for model, hidden in enumerate((ph_ref, rh_ref)):
        base = model * toks
        mixed = hidden[...].astype(f32) + (mixing[base:base + toks] + mixing[rows + base:rows + base + toks])
        scale = lax.rsqrt(jnp.mean(mixed * mixed, axis=1, keepdims=True) + 1e-06)
        normed.append(mixed * scale * gain_ref[...])
    xbuf[pl.ds(here, rows), pl.ds(0, width)] = jnp.concatenate(normed, axis=0).astype(bf16)
    tgt = jnp.broadcast_to(tgt_ref[...], (128, toks))
    kind = lax.broadcasted_iota(jnp.int32, (128, toks), 0)
    digit = jnp.where(kind == 0, tgt & 63, jnp.where(kind == 1, (tgt >> 6) & 63, jnp.where(kind == 2, tgt >> 12, 0)))
    digit = lax.dot_general(same, digit.astype(f32).astype(bf16), NT, preferred_element_type=f32)
    xbuf[pl.ds(here, rows), pl.ds(width, 128)] = jnp.concatenate((digit, digit), axis=0).astype(bf16)

    def view(dx, dy, half, piece):
        where = ((y + dy) % 4) * 4 + (x + dx) % 4
        start, size = ((0, half_w), (half_w, half_w + 128))[half]
        if piece is not None:
            start, size = ((start, quarter), (start + quarter, size - quarter))[piece]
        return xbuf.at[pl.ds(pl.multiple_of(where * rows, 16), rows), pl.ds(start, size)]

    sent += ring_gather(view, lambda dx, dy, nx, ny, half, piece: view(dx, dy, half, piece), near, xsend, xrecv,
                        None, last_pump)
    for k in range(8):
        block = (0, -1, 1, -2, 2, -3, 3, 4)[k]
        ref = hbuf.at[1 - core, (z + block) % zs]
        pltpu.make_async_remote_copy(
            src_ref=ref, dst_ref=ref, send_sem=csend.at[k], recv_sem=crecv.at[k],
            device_id=at(0, 0, 1 - core), device_id_type=MESH).wait_recv()

    stat[slot] = jnp.zeros(stat.shape[1:], f32)
    out_ref[...] = jnp.zeros(out_ref.shape, f32)
    power = lax.broadcasted_iota(jnp.int32, (8, 128), 1)
    power = jnp.where(power == 0, 1.0, jnp.where(power == 1, 64.0, jnp.where(power == 2, 4096.0, 0.0)))
    power = power.astype(bf16)
    tile = 256
    place = lax.broadcasted_iota(jnp.int32, (vrows, tile), 0)

    def tile_body(t, carry):
        rs = pl.ds(pl.multiple_of(t * tile, tile), tile)
        xt = xbuf[rs, pl.ds(0, width)]
        wanted = lax.dot_general(power, xbuf[rs, pl.ds(width, 128)], NT, preferred_element_type=f32)
        wanted = wanted[0:1, :].astype(jnp.int32)

        def block(b, state):
            m, s, p = state
            logits = lax.dot_general(hbuf[b // zs, b % zs], xt, NT, preferred_element_type=f32)
            peak = jnp.maximum(m, jnp.max(logits, axis=0, keepdims=True))
            first = ((b % zs) * (2 * PLANE) + slot * 2 + b // zs) * vrows
            total = s * jnp.exp(m - peak) + jnp.sum(jnp.exp(logits - peak), axis=0, keepdims=True)
            hit = place == (wanted - first)
            got = p + jnp.sum(jnp.where(hit, logits, 0.0), axis=0, keepdims=True)
            return (peak, total, got)

        zero = jnp.zeros((1, tile), f32)
        m, s, p = lax.fori_loop(0, cols, block, (zero - 1e30, zero, zero), unroll=2)
        for k, v in enumerate((m, s, p)):
            stat[slot, k, pl.ds(t * 2, 2), :] = jnp.concatenate([v[:, :128], v[:, 128:]], axis=0)
        return carry

    lax.fori_loop(0, PLANE * rows // tile, tile_body, 0)

    swap = []
    for r in range(1, PLANE):
        cp = pltpu.make_async_remote_copy(
            src_ref=stat.at[slot], dst_ref=stat.at[slot], send_sem=ssend.at[r], recv_sem=srecv.at[r],
            device_id=at(r % 4, r // 4, core), device_id_type=MESH)
        cp.start()
        swap.append(cp)
    index = z * (2 * PLANE) + ep
    number = (lax.broadcasted_iota(jnp.int32, own_ref.shape, 0) * own_ref.shape[1]
              + lax.broadcasted_iota(jnp.int32, own_ref.shape, 1))
    mine = own_ref[...] == index
    lens = len_ref[...].astype(f32)

    def total(v):
        return jnp.sum(jnp.sum(v, axis=0, keepdims=True), axis=1, keepdims=True)

    ordinal = total(jnp.where(mine, number, 0).astype(f32))
    length = total(jnp.where(mine, lens, 0.0))
    first = total(jnp.where(number.astype(f32) < ordinal, lens, 0.0))
    for r in range(1, PLANE):
        source = at(-(r % 4), -(r // 4), core)["ep"] // 2
        pltpu.make_async_remote_copy(
            src_ref=stat.at[source], dst_ref=stat.at[source], send_sem=ssend.at[r], recv_sem=srecv.at[r],
            device_id=at(0, 0, 1 - core), device_id_type=MESH).wait_recv()
    m = stat[0, 0]
    for i in range(1, PLANE):
        m = jnp.maximum(m, stat[i, 0])
    s = jnp.zeros_like(m)
    p = jnp.zeros_like(m)
    for i in range(PLANE):
        s = s + stat[i, 1] * jnp.exp(stat[i, 0] - m)
        p = p + stat[i, 2]
    logprob = p - (m + jnp.log(s))
    lines = PLANE * rows // 128
    flat = jnp.concatenate([logprob[i:i + 1, :] for i in range(lines)], axis=1)
    ratio = flat - pltpu.roll(flat, lines * 128 - toks, 1)
    share[...] = jnp.concatenate([ratio[:, i * 128:(i + 1) * 128] for i in range(lines)]
                                 + [jnp.zeros((16 - lines, 128), f32)], axis=0)
    gath[z * 2 + core] = share[...]
    for j in range(1, cols):
        cp = pltpu.make_async_remote_copy(
            src_ref=share, dst_ref=gath.at[z * 2 + core], send_sem=fsend.at[j], recv_sem=frecv.at[j],
            device_id=col_peer(j), device_id_type=MESH)
        cp.start()
        swap.append(cp)
    out_ref[0:1, :] = pltpu.roll(ratio, (lines * 128 - slot * rows) % (lines * 128), 1)[:, 0:128]
    for j in range(1, cols):
        source = (z * 2 + core + cols - j) % cols
        pltpu.make_async_remote_copy(
            src_ref=share, dst_ref=gath.at[source], send_sem=fsend.at[j], recv_sem=frecv.at[j],
            device_id=col_peer(j), device_id_type=MESH).wait_recv()
    shape = (16, 128)
    spot = lax.broadcasted_iota(jnp.int32, shape, 0) * 128 + lax.broadcasted_iota(jnp.int32, shape, 1)
    from_slot = ((spot.astype(f32) + 0.5) * (1.0 / rows)).astype(jnp.int32)
    rest = spot - from_slot * rows
    live = (rest < toks) & (spot < lines * 128)
    owned = jnp.zeros(shape, f32)
    for i in range(cols):
        position = (((i // 2) * PLANE + from_slot) * 2 + i % 2) * toks + rest
        position = position.astype(f32)
        inside = live & (position >= first) & (position < first + length)
        owned = owned + jnp.where(inside, gath[i], 0.0)
    out_ref[1:2, :] = jnp.broadcast_to(total(owned) / length, (1, 128))
    for cp in sent + returns + ring + swap:
        cp.wait_send()
    for item in across:
        item[4].wait_send()


def local(pol_hidden, ref_hidden, pol_routes, ref_routes, pol_gates, ref_gates, w_gate, w_up, w_down, norm_gain,
          vocab_head, targets, seq_lengths, owners):
    toks, width = pol_hidden.shape
    ff = w_gate.shape[2]
    zs = lax.axis_size("grp")
    vrows = vocab_head.shape[0]
    cols = 2 * zs
    bf16, f32 = jnp.bfloat16, jnp.float32
    vm = pl.BlockSpec(memory_space=pltpu.VMEM)
    hbm = pl.BlockSpec(memory_space=pl.ANY)
    dma = pltpu.SemaphoreType.DMA
    out = pl.pallas_call(
        kernel,
        out_shape=jax.ShapeDtypeStruct((8, 128), f32),
        in_specs=[vm] * 6 + [hbm] * 3 + [vm, hbm] + [vm] * 3,
        out_specs=vm,
        scratch_shapes=[
            pltpu.VMEM((PLANE, 2, 2 * toks + 16, width), bf16),
            pltpu.VMEM((PLANE, 2, 32, width), bf16),
            pltpu.VMEM((2 * PLANE, 32, width), bf16),
            pltpu.VMEM((4 * toks, 2 * PLANE * 32), f32),
            pltpu.VMEM((2, width, ff), bf16),
            pltpu.VMEM((2, width, ff), bf16),
            pltpu.VMEM((2, ff, width), bf16),
            pltpu.VMEM((PLANE * 2 * toks, width + 128), bf16),
            pltpu.VMEM((2, zs, vrows, width), bf16),
            pltpu.VMEM((PLANE, 3, 16, 128), f32),
            pltpu.VMEM((16, 128), f32),
            pltpu.VMEM((cols, 16, 128), f32),
            dma((4,)), dma((40,)), dma((40,)), dma((32,)), dma((32,)), dma((32,)), dma((32,)),
            dma((8,)), dma((8,)), dma((8,)), dma((8,)), dma((40,)), dma((40,)),
            dma((PLANE,)), dma((PLANE,)), dma((cols,)), dma((cols,)),
        ],
        compiler_params=pltpu.CompilerParams(
            collective_id=1, has_side_effects=True, vmem_limit_bytes=62 * 1024 * 1024),
        name="whole",
    )(pol_hidden, ref_hidden, pol_routes.T, ref_routes.T, pol_gates.T, ref_gates.T, w_gate, w_up, w_down,
      norm_gain.reshape(1, width), vocab_head, targets.reshape(1, toks),
      seq_lengths.reshape(-1, 128), owners.reshape(-1, 128))
    return out[0, :toks], out[1, :1]


def solution(mesh):
    return jax.shard_map(
        local,
        mesh=mesh,
        in_specs=(
            P(("grp", "ep"), None),
            P(("grp", "ep"), None),
            P(("grp", "ep"), None),
            P(("grp", "ep"), None),
            P(("grp", "ep"), None),
            P(("grp", "ep"), None),
            P("ep", None, None),
            P("ep", None, None),
            P("ep", None, None),
            P(),
            P(("grp", "ep"), None),
            P(("grp", "ep")),
            P(),
            P(),
        ),
        out_specs=(P(("grp", "ep")), P(("grp", "ep"))),
        check_vma=False,
    )
```
